32 devices in a mesh: dp: 8 (over y, x, core), tensor: 4 (over z).
Axes of the slice: x: 2, y: 2, z: 4, core: 2. Of those that a mesh axis runs over, the one named last changes fastest.
Arguments:
- tokens: bfloat16 [1024, 2048], P('dp', 'tensor'), may hold values from -6 to 6
- grad_out: bfloat16 [1024, 2048], P('dp', 'tensor'), may hold values from -6 to 6
- ln1_gain: float32 [2048], replicated, may hold values from 0.5 to 1.5
- ln1_bias: float32 [2048], replicated, may hold values from -3 to 3
- w_query: bfloat16 [2048, 2048], P(None, 'tensor'), may hold values from -0.13258252 to 0.13258252
- w_key: bfloat16 [2048, 2048], P(None, 'tensor'), may hold values from -0.198873782 to 0.198873782
- w_value: bfloat16 [2048, 3456], P(None, 'tensor'), may hold values from -0.125 to 0.125
- w_gate_ret: bfloat16 [2048, 3456], P(None, 'tensor'), may hold values from -0.125 to 0.125
- w_out: bfloat16 [3456, 2048], P('tensor'), may hold values from -0.15625 to 0.15625
- ln2_gain: float32 [2048], replicated, may hold values from 0.5 to 1.5
- ln2_bias: float32 [2048], replicated, may hold values from -3 to 3
- w_gate_mlp: bfloat16 [2048, 3456], P(None, 'tensor'), may hold values from -0.125 to 0.125
- w_up: bfloat16 [2048, 3456], P(None, 'tensor'), may hold values from -0.125 to 0.125
- w_down: bfloat16 [3456, 2048], P('tensor'), may hold values from -0.15625 to 0.15625
- decay_rate: float32 [8], P('tensor'), may hold values from 0.00048828125 to 0.03125
- seq_lens: int32 [32], replicated, may hold values from 0 to 128, as said below
- seq_owner: int32 [32], replicated, may hold values from 0 to 7
Outputs:
- block_out: float32 [1024, 2048], P('dp', 'tensor')
- grad_tokens: float32 [1024, 2048], P('dp', 'tensor')
- grad_ln1_gain: float32 [2048], replicated
- grad_ln1_bias: float32 [2048], replicated
- grad_w_query: float32 [2048, 2048], P(None, 'tensor')
- grad_w_key: float32 [2048, 2048], P(None, 'tensor')
- grad_w_value: float32 [2048, 3456], P(None, 'tensor')
- grad_w_gate_ret: float32 [2048, 3456], P(None, 'tensor')
- grad_w_out: float32 [3456, 2048], P('tensor')
- grad_ln2_gain: float32 [2048], replicated
- grad_ln2_bias: float32 [2048], replicated
- grad_w_gate_mlp: float32 [2048, 3456], P(None, 'tensor')
- grad_w_up: float32 [2048, 3456], P(None, 'tensor')
- grad_w_down: float32 [3456, 2048], P('tensor')
The draws below stay inside these ranges and needn't reach their ends.
Inputs may be any that keep to these rules, and one draw needn't show every extreme that they name: `seq_lens`: each index of dp owns exactly 4 sequences; the lengths of one index's sequences sum to at most 128, and in every draw some index's sum is exactly 128. A length may be 0.
All inputs are finite; a program needn't handle non-finite values.
Results may differ from the reference program's by a relative error of at most 0.024.
Values may be sent and summed in bfloat16 or wider, within the bound.
No kernel may reach another device: no remote copies, remote signals or barrier semaphores. Data moves between devices by JAX's collectives and lax.ppermute only.
A program may use at most 256 MiB of HBM per device.

```python
import math
import jax
import jax.numpy as jnp
from jax import lax

D = 2048
H = 8
DK = 256
DV = 432
FF = 3456
ROWS = 128
SEQ_DEV = 4
MAXLEN = 512
V = 3456
TOKENS = 1024
N_DP = 8
N_TENSOR = 4


def sequence_plan(key):
    owner_key = jax.random.fold_in(key, 11)
    length_key = jax.random.fold_in(key, 12)
    full_key = jax.random.fold_in(key, 13)
    total_seq = SEQ_DEV * N_DP
    base_owner = jnp.arange(total_seq, dtype=jnp.int32) // SEQ_DEV
    seq_owner = jax.random.permutation(owner_key, base_owner).astype(jnp.int32)
    cap_len = min(MAXLEN, ROWS // 4)
    len_table = jax.random.randint(length_key, (N_DP, SEQ_DEV), 0, cap_len + 1, dtype=jnp.int32)
    full_dev = jax.random.randint(full_key, (), 0, N_DP, dtype=jnp.int32)
    first_len = min(MAXLEN, ROWS)
    slot_ids = jnp.arange(SEQ_DEV, dtype=jnp.int32)
    full_row = jnp.where(slot_ids == 0, first_len, jnp.where(slot_ids == 1, ROWS - first_len, 0)).astype(jnp.int32)
    is_full = (jnp.arange(N_DP, dtype=jnp.int32) == full_dev)[:, None]
    len_table = jnp.where(is_full, full_row[None, :], len_table)
    seq_ids = jnp.arange(total_seq, dtype=jnp.int32)
    earlier = (seq_ids[None, :] < seq_ids[:, None]) & (seq_owner[None, :] == seq_owner[:, None])
    seq_rank = jnp.sum(earlier.astype(jnp.int32), axis=1, dtype=jnp.int32)
    lengths = len_table[seq_owner, seq_rank]
    return (lengths.astype(jnp.int32), seq_owner)


def draw_seq_lens(key, part):
    return sequence_plan(key)[0]


def draw_seq_owner(key, part):
    return sequence_plan(key)[1]


def projection_pair(key):
    shared_key = jax.random.fold_in(key, 21)
    own_key = jax.random.fold_in(key, 22)
    shape = (D, H * DK)
    shared = jnp.clip(jax.random.normal(shared_key, shape, dtype=jnp.float32), -6.0, 6.0)
    own = jnp.clip(jax.random.normal(own_key, shape, dtype=jnp.float32), -6.0, 6.0)
    scale = D ** (-0.5)
    query_part = shared * scale
    key_part = (shared + 0.5 * own) * (scale / 1.25 ** 0.5)
    return (query_part, key_part)


def draw_w_query(key, part):
    return projection_pair(key)[0].astype(jnp.bfloat16)


def draw_w_key(key, part):
    return projection_pair(key)[1].astype(jnp.bfloat16)


def block_scale(key, shape, split, smallest, high):
    level, own = 1.0, jax.random.fold_in(key, 6)
    for axis_at, blocks in split:
        draws = jnp.exp(jax.random.uniform(jax.random.fold_in(own, axis_at), (blocks,), jnp.float32, smallest / len(split), high / len(split)))
        level = level * jnp.repeat(draws, shape[axis_at] // blocks).reshape([-1 if axis == axis_at else 1 for axis in range(len(shape))])
    return level


def noise(rng, dims, deviation, limit, split=(), held_as=jnp.bfloat16):
    values = jax.random.normal(rng, dims, jnp.float32) * deviation
    if len(split) > 0:
        values = block_scale(rng, dims, split, -0.22, 0.18) * values
    return jnp.clip(values, min=-limit, max=limit).astype(held_as)


def setup_inputs(seed: int = 0) -> dict:
    seeds = jax.random.split(jax.random.key(seed), 18)
    return {
        "tokens": noise(seeds[0], (TOKENS, D), 1.0, 6.0, ((0, 8), (1, 4))),
        "grad_out": noise(seeds[1], (TOKENS, D), 1.0, 6.0, ((0, 8), (1, 4))),
        "ln1_gain": jnp.clip(1.0 + 0.1 * jax.random.normal(seeds[2], (D,), jnp.float32), 0.5, 1.5),
        "ln1_bias": noise(seeds[3], (D,), 0.5, 3.0, (), jnp.float32),
        "w_query": draw_w_query(jax.random.fold_in(seeds[17], 71), 0),
        "w_key": draw_w_key(jax.random.fold_in(seeds[17], 71), 0),
        "w_value": noise(seeds[6], (D, V), D ** -0.5, 0.125, ((1, 4),)),
        "w_gate_ret": noise(seeds[7], (D, V), D ** -0.5, 0.125, ((1, 4),)),
        "w_out": noise(seeds[8], (V, D), (V // 2) ** -0.5, 0.15625, ((0, 4),)),
        "ln2_gain": jnp.clip(1.0 + 0.1 * jax.random.normal(seeds[9], (D,), jnp.float32), 0.5, 1.5),
        "ln2_bias": noise(seeds[10], (D,), 0.5, 3.0, (), jnp.float32),
        "w_gate_mlp": noise(seeds[11], (D, FF), D ** -0.5, 0.125, ((1, 4),)),
        "w_up": noise(seeds[12], (D, FF), D ** -0.5, 0.125, ((1, 4),)),
        "w_down": noise(seeds[13], (FF, D), (FF // 2) ** -0.5, 0.15625, ((0, 4),)),
        "decay_rate": jnp.clip(jnp.exp(math.log(0.03125) - 4.158883 * jax.random.uniform(seeds[14], (H,), jnp.float32) ** block_scale(seeds[14], (H,), ((0, 4),), -0.2, 0.2)), 0.00048828125, 0.03125),
        "seq_lens": draw_seq_lens(jax.random.fold_in(seeds[17], 71), 0),
        "seq_owner": draw_seq_owner(jax.random.fold_in(seeds[17], 71), 0),
    }


norm_eps = 1e-05

def layout(seq_lens, seq_owner, device, row_count):
    owned_mask = (seq_owner == device).astype(jnp.int32)
    seq_count = seq_lens * owned_mask
    starts = jnp.cumsum(seq_count, dtype=jnp.int32) - seq_count
    row_ids = jnp.arange(row_count, dtype=jnp.int32)[:, None]
    inside = ((row_ids >= starts[None, :]) & (row_ids < (starts + seq_count)[None, :])).astype(jnp.int32)
    seq_numbers = jnp.arange(seq_count.shape[0], dtype=jnp.int32)
    segment = lax.optimization_barrier(jnp.sum(inside * (seq_numbers[None, :] + 1), axis=1, dtype=jnp.int32)) - 1
    position = lax.optimization_barrier(jnp.sum(inside * (row_ids - starts[None, :]), axis=1, dtype=jnp.int32))
    return (segment, position)

def layer_norm(values, norm_gain, norm_bias):
    row_mean = lax.optimization_barrier(jnp.mean(values, axis=-1, keepdims=True))
    centred = values - row_mean
    variance = lax.optimization_barrier(jnp.mean(centred * centred, axis=-1, keepdims=True))
    inv_std = lax.rsqrt(variance + norm_eps)
    norm_hat = centred * inv_std
    return (norm_hat * norm_gain + norm_bias, norm_hat, inv_std)

def group_norm(values):
    row_mean = lax.optimization_barrier(jnp.mean(values, axis=-1, keepdims=True))
    centred = values - row_mean
    variance = lax.optimization_barrier(jnp.mean(centred * centred, axis=-1, keepdims=True))
    inv_std = lax.rsqrt(variance + norm_eps)
    return (centred * inv_std, inv_std)

def norm_back(upstream, norm_hat, inv_std):
    first_mean = lax.optimization_barrier(jnp.mean(upstream, axis=-1, keepdims=True))
    second_mean = lax.optimization_barrier(jnp.mean(upstream * norm_hat, axis=-1, keepdims=True))
    return inv_std * (upstream - first_mean - norm_hat * second_mean)

def xpos_tables(position, half_dim):
    freq_index = jnp.arange(half_dim, dtype=jnp.float32)
    angle_rate = 10000.0 ** (-freq_index / half_dim)
    zeta_base = (freq_index / half_dim + 0.4) / 1.4
    pos_col = position.astype(jnp.float32)[:, None]
    angles = pos_col * angle_rate[None, :]
    growth = jnp.exp(jnp.log(zeta_base)[None, :] * pos_col / 512.0)
    return (jnp.cos(angles)[:, None, :], jnp.sin(angles)[:, None, :], growth[:, None, :])

def apply_rotation(heads, cosine, sine, factor):
    half_dim = heads.shape[-1] // 2
    lower_half = heads[..., :half_dim]
    upper_half = heads[..., half_dim:]
    return jnp.concatenate([(lower_half * cosine - upper_half * sine) * factor, (lower_half * sine + upper_half * cosine) * factor], axis=-1)

def rotate_back(grads, cosine, sine, factor):
    half_dim = grads.shape[-1] // 2
    lower_half = grads[..., :half_dim]
    upper_half = grads[..., half_dim:]
    return jnp.concatenate([(lower_half * cosine + upper_half * sine) * factor, (upper_half * cosine - lower_half * sine) * factor], axis=-1)

def decay_mask(segment, position, rates):
    row_count = segment.shape[0]
    same_seq = (segment[:, None] == segment[None, :]) & (segment[:, None] >= 0)
    row_ids = jnp.arange(row_count, dtype=jnp.int32)
    allowed = same_seq & (row_ids[:, None] >= row_ids[None, :])
    distance = jnp.where(allowed, (position[:, None] - position[None, :]).astype(jnp.float32), 0.0)
    return jnp.where(allowed[None], jnp.exp(-rates[:, None, None] * distance[None]), 0.0)

def silu_gate(pre_act, other):
    return jax.nn.silu(pre_act) * other

def gelu_gate(pre_act, other):
    return jax.nn.gelu(pre_act, approximate=True) * other

def group_sum(parts):
    rounded = lax.optimization_barrier(parts.astype(jnp.bfloat16))
    return lax.optimization_barrier(jnp.sum(rounded.astype(jnp.float32), axis=0))

def split_product(left, right, groups):
    row_count = left.shape[0]
    inner = left.shape[1] // groups
    left_groups = left.astype(jnp.float32).reshape(row_count, groups, inner)
    right_groups = right.astype(jnp.float32).reshape(groups, inner, right.shape[1])
    return jnp.einsum('rtk,tkd->trd', left_groups, right_groups)

def split_back(grads, weight, groups):
    row_count = grads.shape[0]
    inner = grads.shape[1] // groups
    grad_groups = grads.astype(jnp.float32).reshape(row_count, groups, inner)
    weight_groups = weight.astype(jnp.float32).reshape(weight.shape[0], groups, inner)
    return jnp.einsum('rtk,dtk->trd', grad_groups, weight_groups)

def mm(left, right):
    return jnp.dot(left, right, preferred_element_type=jnp.float32)

def reference(tokens, grad_out, ln1_gain, ln1_bias, w_query, w_key, w_value, w_gate_ret, w_out, ln2_gain, ln2_bias, w_gate_mlp, w_up, w_down, decay_rate, seq_lens, seq_owner):
    groups = N_TENSOR

    def one_block(totals, item):
        token_blk, grad_blk, block_id = item
        segment, position = layout(seq_lens, seq_owner, block_id, ROWS)
        live = segment >= 0
        x_wide = token_blk.astype(jnp.float32)
        normed1, hat_one, inv_one = layer_norm(x_wide, ln1_gain, ln1_bias)
        act_one = normed1.astype(jnp.bfloat16)
        query = mm(act_one, w_query)
        keys = mm(act_one, w_key)
        values = mm(act_one, w_value)
        gate_pre = mm(act_one, w_gate_ret)
        cosine, sine, growth = xpos_tables(position, DK // 2)
        key_factor = 1.0 / growth * DK ** (-0.5)
        rotated_query = apply_rotation(query.reshape(ROWS, H, DK), cosine, sine, growth).astype(jnp.bfloat16)
        rotated_key = apply_rotation(keys.reshape(ROWS, H, DK), cosine, sine, key_factor).astype(jnp.bfloat16)
        value_b = values.reshape(ROWS, H, DV).astype(jnp.bfloat16)
        mask = decay_mask(segment, position, decay_rate)
        retention_scores = jnp.einsum('sqp,fqp->qsf', rotated_query.astype(jnp.float32), rotated_key.astype(jnp.float32))
        weights_b = (retention_scores * mask).astype(jnp.bfloat16)
        retained = jnp.einsum('hrm,mhv->rhv', weights_b.astype(jnp.float32), value_b.astype(jnp.float32))
        y_norm, inv_group = group_norm(retained)
        y_flat = y_norm.reshape(ROWS, H * DV)
        gated = silu_gate(gate_pre, y_flat).astype(jnp.bfloat16)
        resid = x_wide + group_sum(split_product(gated, w_out, groups))
        normed2, hat_two, inv_two = layer_norm(resid, ln2_gain, ln2_bias)
        act_two = normed2.astype(jnp.bfloat16)
        up_gate = mm(act_two, w_gate_mlp)
        up_lin = mm(act_two, w_up)
        hidden = gelu_gate(up_gate, up_lin).astype(jnp.bfloat16)
        block_out = resid + group_sum(split_product(hidden, w_down, groups))
        grad_active_rows = jnp.where(live[:, None], grad_blk, jnp.zeros_like(grad_blk))
        grad_wide = grad_active_rows.astype(jnp.float32)
        grad_down = mm(hidden.T, grad_active_rows)
        back_hidden = mm(grad_active_rows, w_down.T)
        gelu_vjp = jax.vjp(gelu_gate, up_gate, up_lin)[1]
        back_gate_mlp, back_up = gelu_vjp(back_hidden)
        back_gate_mlp = back_gate_mlp.astype(jnp.bfloat16)
        back_up = back_up.astype(jnp.bfloat16)
        grad_gate_mlp = mm(act_two.T, back_gate_mlp)
        grad_up = mm(act_two.T, back_up)
        back_act_two = group_sum(split_back(back_gate_mlp, w_gate_mlp, groups) + split_back(back_up, w_up, groups))
        grad_ln2_gain = lax.optimization_barrier(jnp.sum(back_act_two * hat_two, axis=0))
        grad_ln2_bias = lax.optimization_barrier(jnp.sum(back_act_two, axis=0))
        back_resid = grad_wide + norm_back(back_act_two * ln2_gain, hat_two, inv_two)
        resid_b = back_resid.astype(jnp.bfloat16)
        grad_out_w = mm(gated.T, resid_b)
        back_gated = mm(resid_b, w_out.T)
        silu_vjp = jax.vjp(silu_gate, gate_pre, y_flat)[1]
        back_gate_pre, back_y = silu_vjp(back_gated)
        gate_b = back_gate_pre.astype(jnp.bfloat16)
        back_ret = norm_back(back_y.reshape(ROWS, H, DV), y_norm, inv_group).astype(jnp.bfloat16)
        grad_retention_weights = (jnp.einsum('rhv,mhv->hrm', back_ret.astype(jnp.float32), value_b.astype(jnp.float32)) * mask).astype(jnp.bfloat16)
        back_value = jnp.einsum('hrm,rhv->mhv', weights_b.astype(jnp.float32), back_ret.astype(jnp.float32)).astype(jnp.bfloat16).reshape(ROWS, H * DV)
        grad_rotated_query = jnp.einsum('zve,ezk->vzk', grad_retention_weights.astype(jnp.float32), rotated_key.astype(jnp.float32))
        grad_rotated_key = jnp.einsum('glv,lgc->vgc', grad_retention_weights.astype(jnp.float32), rotated_query.astype(jnp.float32))
        back_query = rotate_back(grad_rotated_query, cosine, sine, growth).astype(jnp.bfloat16).reshape(ROWS, H * DK)
        back_key = rotate_back(grad_rotated_key, cosine, sine, key_factor).astype(jnp.bfloat16).reshape(ROWS, H * DK)
        grad_q = mm(act_one.T, back_query)
        grad_k = mm(act_one.T, back_key)
        grad_v = mm(act_one.T, back_value)
        grad_g = mm(act_one.T, gate_b)
        partial_one = split_back(back_query, w_query, groups) + split_back(back_key, w_key, groups)
        partial_one = partial_one + split_back(back_value, w_value, groups) + split_back(gate_b, w_gate_ret, groups)
        back_act_one = group_sum(partial_one)
        grad_ln1_gain = lax.optimization_barrier(jnp.sum(back_act_one * hat_one, axis=0))
        grad_ln1_bias = lax.optimization_barrier(jnp.sum(back_act_one, axis=0))
        grad_tokens = back_resid + norm_back(back_act_one * ln1_gain, hat_one, inv_one)
        grads = (grad_ln1_gain, grad_ln1_bias, grad_q, grad_k, grad_v, grad_g, grad_out_w, grad_ln2_gain, grad_ln2_bias, grad_gate_mlp, grad_up, grad_down)
        return (jax.tree.map(jnp.add, totals, grads), (block_out, grad_tokens))
    zeros_init = (jnp.zeros((D,), jnp.float32), jnp.zeros((D,), jnp.float32), jnp.zeros((D, H * DK), jnp.float32), jnp.zeros((D, H * DK), jnp.float32), jnp.zeros((D, H * DV), jnp.float32), jnp.zeros((D, H * DV), jnp.float32), jnp.zeros((H * DV, D), jnp.float32), jnp.zeros((D,), jnp.float32), jnp.zeros((D,), jnp.float32), jnp.zeros((D, FF), jnp.float32), jnp.zeros((D, FF), jnp.float32), jnp.zeros((FF, D), jnp.float32))
    blocks_x = tokens.reshape(N_DP, ROWS, D)
    blocks_g = grad_out.reshape(N_DP, ROWS, D)
    block_ids = jnp.arange(N_DP, dtype=jnp.int32)
    totals, stacked = lax.scan(one_block, zeros_init, (blocks_x, blocks_g, block_ids))
    block_out = stacked[0].reshape(N_DP * ROWS, D)
    grad_tokens = stacked[1].reshape(N_DP * ROWS, D)
    return (block_out, grad_tokens, totals[0], totals[1], totals[2], totals[3], totals[4], totals[5], totals[6], totals[7], totals[8], totals[9], totals[10], totals[11])
```

```python
import functools

import jax
import jax.numpy as jnp
from jax import lax
from jax.experimental import pallas as pl
from jax.experimental.pallas import tpu as pltpu
from jax.sharding import PartitionSpec as P

norm_eps = 1e-05


def layout(seq_lens, seq_owner, device, row_count):
    owned_mask = (seq_owner == device).astype(jnp.int32)
    seq_count = seq_lens * owned_mask
    starts = jnp.cumsum(seq_count, dtype=jnp.int32) - seq_count
    row_ids = jnp.arange(row_count, dtype=jnp.int32)[:, None]
    inside = ((row_ids >= starts[None, :]) & (row_ids < (starts + seq_count)[None, :])).astype(
        jnp.int32
    )
    seq_numbers = jnp.arange(seq_count.shape[0], dtype=jnp.int32)
    segment = jnp.sum(inside * (seq_numbers[None, :] + 1), axis=1, dtype=jnp.int32) - 1
    position = jnp.sum(inside * (row_ids - starts[None, :]), axis=1, dtype=jnp.int32)
    return (segment, position)


def layer_norm(values, norm_gain, norm_bias):
    row_mean = jnp.mean(values, axis=-1, keepdims=True)
    centred = values - row_mean
    variance = jnp.mean(centred * centred, axis=-1, keepdims=True)
    inv_std = lax.rsqrt(variance + norm_eps)
    norm_hat = centred * inv_std
    return (norm_hat * norm_gain + norm_bias, norm_hat, inv_std)


def group_norm(values):
    row_mean = jnp.mean(values, axis=-1, keepdims=True)
    centred = values - row_mean
    variance = jnp.mean(centred * centred, axis=-1, keepdims=True)
    inv_std = lax.rsqrt(variance + norm_eps)
    return (centred * inv_std, inv_std)


def norm_back(upstream, norm_hat, inv_std):
    first_mean = jnp.mean(upstream, axis=-1, keepdims=True)
    second_mean = jnp.mean(upstream * norm_hat, axis=-1, keepdims=True)
    return inv_std * (upstream - first_mean - norm_hat * second_mean)


def xpos_tables(position, half_dim):
    freq_index = jnp.arange(half_dim, dtype=jnp.float32)
    angle_rate = 10000.0 ** (-freq_index / half_dim)
    zeta_base = (freq_index / half_dim + 0.4) / 1.4
    pos_col = position.astype(jnp.float32)[:, None]
    angles = pos_col * angle_rate[None, :]
    growth = jnp.exp(jnp.log(zeta_base)[None, :] * pos_col / 512.0)
    return (jnp.cos(angles)[:, None, :], jnp.sin(angles)[:, None, :], growth[:, None, :])


def apply_rotation(heads, cosine, sine, factor):
    half_dim = heads.shape[-1] // 2
    lower_half = heads[..., :half_dim]
    upper_half = heads[..., half_dim:]
    return jnp.concatenate(
        [
            (lower_half * cosine - upper_half * sine) * factor,
            (lower_half * sine + upper_half * cosine) * factor,
        ],
        axis=-1,
    )


def rotate_back(grads, cosine, sine, factor):
    half_dim = grads.shape[-1] // 2
    lower_half = grads[..., :half_dim]
    upper_half = grads[..., half_dim:]
    return jnp.concatenate(
        [
            (lower_half * cosine + upper_half * sine) * factor,
            (upper_half * cosine - lower_half * sine) * factor,
        ],
        axis=-1,
    )


def decay_mask(segment, position, rates):
    row_count = segment.shape[0]
    same_seq = (segment[:, None] == segment[None, :]) & (segment[:, None] >= 0)
    row_ids = jnp.arange(row_count, dtype=jnp.int32)
    allowed = same_seq & (row_ids[:, None] >= row_ids[None, :])
    distance = jnp.where(allowed, (position[:, None] - position[None, :]).astype(jnp.float32), 0.0)
    return jnp.where(allowed[None], jnp.exp(-rates[:, None, None] * distance[None]), 0.0)


def silu_gate(pre_act, other):
    return jax.nn.silu(pre_act) * other


def gelu_gate(pre_act, other):
    return jax.nn.gelu(pre_act, approximate=True) * other


def matmul(left, right):
    return jnp.dot(left, right, preferred_element_type=jnp.float32)


both_axes = ("dp", "tensor")


def swap_perm(dp_size, tensor_size, dp_masks, tensor_masks):
    pairs = []
    for dp_at in range(dp_size):
        core = dp_at % 2
        for t_at in range(tensor_size):
            source = dp_at * tensor_size + t_at
            target = (dp_at ^ dp_masks[core]) * tensor_size + (t_at ^ tensor_masks[core])
            pairs.append((source, target))
    return pairs


class Wires:
    def __init__(self, dp_size, tensor_size):
        self.dp_size, self.tensor_size = dp_size, tensor_size
        make = functools.partial(swap_perm, dp_size, tensor_size)
        self.ring = tensor_size == 4 and dp_size % 2 == 0
        self.square = dp_size == 8
        self.z_first, self.z_second = make((0, 0), (1, 3)), make((0, 0), (3, 1))
        self.xy_first, self.xy_second = make((2, 4), (0, 0)), make((4, 2), (0, 0))
        self.x_only, self.y_only = make((2, 2), (0, 0)), make((4, 4), (0, 0))
        self.core = make((1, 1), (0, 0))

    def gather_columns(self, shard):
        if not self.ring:
            return lax.all_gather(shard, "tensor", axis=1, tiled=True)
        t_at = lax.axis_index("tensor")
        core = lax.axis_index("dp") % 2
        first = lax.ppermute(shard, both_axes, self.z_first)
        second = lax.ppermute(shard, both_axes, self.z_second)
        far = lax.ppermute(first, both_axes, self.z_second)
        near = t_at ^ jnp.where(core == 0, 1, 3)
        other = t_at ^ jnp.where(core == 0, 3, 1)
        width = shard.shape[1]
        full = jnp.zeros((shard.shape[0], width * 4), shard.dtype)
        for piece, at in ((shard, t_at), (first, near), (second, other), (far, t_at ^ 2)):
            full = lax.dynamic_update_slice_in_dim(full, piece, at * width, 1)
        return full

    def sum_over_tensor(self, part):
        if not self.ring:
            return lax.psum(part.astype(jnp.bfloat16), "tensor").astype(jnp.float32)
        mine = part.astype(jnp.bfloat16)
        other = lax.ppermute(mine, both_axes, self.z_first)
        pair = (mine.astype(jnp.float32) + other.astype(jnp.float32)).astype(jnp.bfloat16)
        far = lax.ppermute(pair, both_axes, self.z_second)
        return pair.astype(jnp.float32) + far.astype(jnp.float32)

    def scatter_columns(self, part):
        mine = part.astype(jnp.bfloat16)
        if not self.ring:
            return lax.psum_scatter(mine, "tensor", scatter_dimension=1, tiled=True).astype(jnp.float32)
        t_at = lax.axis_index("tensor")
        width = part.shape[1] // 4
        total = lax.dynamic_slice_in_dim(mine, t_at * width, width, 1).astype(jnp.float32)
        for mask in (1, 3, 2):
            block = lax.dynamic_slice_in_dim(mine, (t_at ^ mask) * width, width, 1)
            pairs = [(at, at ^ mask) for at in range(4)]
            total = total + lax.ppermute(block, "tensor", pairs).astype(jnp.float32)
        return total

    def rows_of_all(self, block):
        if not self.square:
            stacked = lax.all_gather(block, "dp", axis=0, tiled=False)
            return [stacked[at] for at in range(self.dp_size)]
        first = lax.ppermute(block, both_axes, self.xy_first)
        second = lax.ppermute(block, both_axes, self.xy_second)
        far = lax.ppermute(first, both_axes, self.xy_second)
        near = [block, first, second, far]
        return near + [lax.ppermute(piece, both_axes, self.core) for piece in near]

    def sum_small(self, vector):
        if not self.square:
            return lax.psum(vector, "dp")
        for pairs in (self.core, self.x_only, self.y_only):
            vector = vector + lax.ppermute(vector, both_axes, pairs)
        return vector


def rows_kernel(count, tile, *refs):
    lefts, rights, outs = refs[:count], refs[count : 2 * count], refs[2 * count :]
    right = jnp.concatenate([ref[...] for ref in rights], axis=0)
    offset = 0
    for out in outs:
        height = out.shape[0]
        for row in range(0, height, tile):
            rows = slice(offset + row, offset + row + tile)
            left = jnp.concatenate([ref[rows, :] for ref in lefts], axis=1)
            out[row : row + tile, :] = jnp.dot(left, right, preferred_element_type=jnp.float32)
        offset += height


def weight_grad_rows(lefts, rights, heights):
    count = len(lefts)
    total, rows = lefts[0].shape
    width = rights[0].shape[1]
    tile = 288 if heights[0] % 288 == 0 else heights[0] // 3 if heights[0] % 48 == 0 else heights[0]
    step = min(512, width)
    return pl.pallas_call(
        functools.partial(rows_kernel, count, tile),
        grid=(width // step,),
        in_specs=[pl.BlockSpec((total, rows), lambda j: (0, 0), pipeline_mode=pl.Buffered(1))] * count
        + [pl.BlockSpec((rows, step), lambda j: (0, j))] * count,
        out_specs=[pl.BlockSpec((height, step), lambda j: (0, j)) for height in heights],
        out_shape=[jax.ShapeDtypeStruct((height, width), jnp.float32) for height in heights],
        compiler_params=pltpu.CompilerParams(vmem_limit_bytes=52 * 2**20),
        cost_estimate=pl.CostEstimate(
            flops=2 * total * rows * count * width,
            bytes_accessed=count * rows * (total + width) * 2 + total * width * 4,
            transcendentals=0,
        ),
    )(*lefts, *rights)


def columns_kernel(count, *refs):
    lefts, rights, outs = refs[:count], refs[count : 2 * count], refs[2 * count :]
    left = jnp.concatenate([ref[...] for ref in lefts], axis=0)
    offset = 0
    for out in outs:
        width = out.shape[1]
        right = jnp.concatenate([ref[:, offset : offset + width] for ref in rights], axis=0)
        out[...] = lax.dot_general(left, right, (((0,), (0,)), ((), ())), preferred_element_type=jnp.float32)
        offset += width


def weight_grad_columns(lefts, rights, widths):
    count = len(lefts)
    rows, height = lefts[0].shape
    total = rights[0].shape[1]
    step = min(512, height)
    return pl.pallas_call(
        functools.partial(columns_kernel, count),
        grid=(height // step,),
        in_specs=[pl.BlockSpec((rows, step), lambda j: (0, j))] * count
        + [pl.BlockSpec((rows, total), lambda j: (0, 0), pipeline_mode=pl.Buffered(1))] * count,
        out_specs=[pl.BlockSpec((step, width), lambda j: (j, 0)) for width in widths],
        out_shape=[jax.ShapeDtypeStruct((height, width), jnp.float32) for width in widths],
        compiler_params=pltpu.CompilerParams(vmem_limit_bytes=52 * 2**20),
        cost_estimate=pl.CostEstimate(
            flops=2 * total * rows * count * height,
            bytes_accessed=count * rows * (total + height) * 2 + total * height * 4,
            transcendentals=0,
        ),
    )(*lefts, *rights)


def local(
    wires,
    tokens,
    grad_out,
    ln1_gain,
    ln1_bias,
    w_query,
    w_key,
    w_value,
    w_gate_ret,
    w_out,
    ln2_gain,
    ln2_bias,
    w_gate_mlp,
    w_up,
    w_down,
    decay_rate,
    seq_lens,
    seq_owner,
):
    row_count = tokens.shape[0]
    col_count = tokens.shape[1]
    local_heads = decay_rate.shape[0]
    key_dim = w_query.shape[1] // local_heads
    val_dim = w_value.shape[1] // local_heads
    col_start = lax.axis_index("tensor") * col_count
    segment, position = layout(seq_lens, seq_owner, lax.axis_index("dp"), row_count)
    live = segment >= 0
    x_full = wires.gather_columns(tokens)
    grad_active_rows = wires.gather_columns(jnp.where(live[:, None], grad_out, jnp.zeros_like(grad_out)))
    grad_all = wires.rows_of_all(grad_active_rows)
    x_wide = x_full.astype(jnp.float32)
    normed1, hat_one, inv_one = layer_norm(x_wide, ln1_gain, ln1_bias)
    act_one = normed1.astype(jnp.bfloat16)
    act_one_all = wires.rows_of_all(act_one)
    query = matmul(act_one, w_query)
    keys = matmul(act_one, w_key)
    values = matmul(act_one, w_value)
    gate_pre = matmul(act_one, w_gate_ret)
    cosine, sine, growth = xpos_tables(position, key_dim // 2)
    key_factor = 1.0 / growth * key_dim ** (-0.5)
    rotated_query = apply_rotation(
        query.reshape(row_count, local_heads, key_dim), cosine, sine, growth
    ).astype(jnp.bfloat16)
    rotated_key = apply_rotation(
        keys.reshape(row_count, local_heads, key_dim), cosine, sine, key_factor
    ).astype(jnp.bfloat16)
    value_b = values.reshape(row_count, local_heads, val_dim).astype(jnp.bfloat16)
    mask = decay_mask(segment, position, decay_rate)
    retention_scores = jnp.einsum(
        "sqp,fqp->qsf", rotated_query, rotated_key, preferred_element_type=jnp.float32
    )
    weights_b = (retention_scores * mask).astype(jnp.bfloat16)
    retained = jnp.einsum("hrm,mhv->rhv", weights_b, value_b, preferred_element_type=jnp.float32)
    y_norm, inv_group = group_norm(retained)
    y_flat = y_norm.reshape(row_count, local_heads * val_dim)
    gated = silu_gate(gate_pre, y_flat).astype(jnp.bfloat16)
    out_part = matmul(gated, w_out)
    gated_all = wires.rows_of_all(gated.T)
    attn_full = wires.sum_over_tensor(out_part)
    resid_full = x_wide + attn_full
    resid_cols = lax.dynamic_slice_in_dim(resid_full, col_start, col_count, 1)
    normed2, hat_two, inv_two = layer_norm(resid_full, ln2_gain, ln2_bias)
    act_two = normed2.astype(jnp.bfloat16)
    act_two_all = wires.rows_of_all(act_two)
    up_gate = matmul(act_two, w_gate_mlp)
    up_lin = matmul(act_two, w_up)
    hidden = gelu_gate(up_gate, up_lin).astype(jnp.bfloat16)
    mlp_part = matmul(hidden, w_down)
    mlp_cols = wires.scatter_columns(mlp_part)
    block_out = resid_cols + mlp_cols
    grad_wide = grad_active_rows.astype(jnp.float32)
    back_hidden = matmul(grad_active_rows, w_down.T)
    gelu_vjp = jax.vjp(gelu_gate, up_gate, up_lin)[1]
    back_gate_mlp, back_up = gelu_vjp(back_hidden)
    back_gate_mlp = back_gate_mlp.astype(jnp.bfloat16)
    back_up = back_up.astype(jnp.bfloat16)
    ff = hidden.shape[1]
    mlp_all = wires.rows_of_all(jnp.concatenate([hidden.T, back_gate_mlp.T, back_up.T], axis=0))
    (grad_down,) = weight_grad_rows([piece[:ff] for piece in mlp_all], grad_all, (ff,))
    grad_gate_mlp, grad_up = weight_grad_rows([piece[ff:] for piece in mlp_all], act_two_all, (ff, ff))
    grad_gate_mlp, grad_up = grad_gate_mlp.T, grad_up.T
    partial_two = matmul(back_gate_mlp, w_gate_mlp.T) + matmul(back_up, w_up.T)
    back_act_two = wires.sum_over_tensor(partial_two)
    grad_ln2_gain = jnp.sum(back_act_two * hat_two, axis=0)
    grad_ln2_bias = jnp.sum(back_act_two, axis=0)
    back_resid = grad_wide + norm_back(back_act_two * ln2_gain, hat_two, inv_two)
    resid_b = back_resid.astype(jnp.bfloat16)
    resid_all = wires.rows_of_all(resid_b)
    (grad_out_w,) = weight_grad_rows(gated_all, resid_all, (gated.shape[1],))
    back_gated = matmul(resid_b, w_out.T)
    silu_vjp = jax.vjp(silu_gate, gate_pre, y_flat)[1]
    back_gate_pre, back_y = silu_vjp(back_gated)
    gate_b = back_gate_pre.astype(jnp.bfloat16)
    back_ret = norm_back(back_y.reshape(row_count, local_heads, val_dim), y_norm, inv_group).astype(
        jnp.bfloat16
    )
    grad_retention_weights = (
        jnp.einsum("rhv,mhv->hrm", back_ret, value_b, preferred_element_type=jnp.float32) * mask
    ).astype(jnp.bfloat16)
    back_value = (
        jnp.einsum("hrm,rhv->mhv", weights_b, back_ret, preferred_element_type=jnp.float32)
        .astype(jnp.bfloat16)
        .reshape(row_count, local_heads * val_dim)
    )
    grad_rotated_query = jnp.einsum(
        "zve,ezk->vzk", grad_retention_weights, rotated_key, preferred_element_type=jnp.float32
    )
    grad_rotated_key = jnp.einsum(
        "glv,lgc->vgc", grad_retention_weights, rotated_query, preferred_element_type=jnp.float32
    )
    back_query = (
        rotate_back(grad_rotated_query, cosine, sine, growth)
        .astype(jnp.bfloat16)
        .reshape(row_count, local_heads * key_dim)
    )
    back_key = (
        rotate_back(grad_rotated_key, cosine, sine, key_factor)
        .astype(jnp.bfloat16)
        .reshape(row_count, local_heads * key_dim)
    )
    wide_all = wires.rows_of_all(jnp.concatenate([back_value.T, gate_b.T], axis=0))
    narrow_all = wires.rows_of_all(jnp.concatenate([back_query, back_key], axis=1))
    vals = back_value.shape[1]
    grad_v, grad_g = weight_grad_rows(wide_all, act_one_all, (vals, vals))
    grad_v, grad_g = grad_v.T, grad_g.T
    width = back_query.shape[1]
    grad_q, grad_k = weight_grad_columns(act_one_all, narrow_all, (width, width))
    partial_one = matmul(back_query, w_query.T) + matmul(back_key, w_key.T)
    partial_one = partial_one + matmul(back_value, w_value.T) + matmul(gate_b, w_gate_ret.T)
    back_act_one = wires.sum_over_tensor(partial_one)
    grad_ln1_gain = jnp.sum(back_act_one * hat_one, axis=0)
    grad_ln1_bias = jnp.sum(back_act_one, axis=0)
    back_tokens = back_resid + norm_back(back_act_one * ln1_gain, hat_one, inv_one)
    grad_tokens = lax.dynamic_slice_in_dim(back_tokens, col_start, col_count, 1)
    grad_ln2_gain, grad_ln2_bias = wires.sum_small(jnp.stack([grad_ln2_gain, grad_ln2_bias]))
    grad_ln1_gain, grad_ln1_bias = wires.sum_small(jnp.stack([grad_ln1_gain, grad_ln1_bias]))
    return (
        block_out,
        grad_tokens,
        grad_ln1_gain,
        grad_ln1_bias,
        grad_q,
        grad_k,
        grad_v,
        grad_g,
        grad_out_w,
        grad_ln2_gain,
        grad_ln2_bias,
        grad_gate_mlp,
        grad_up,
        grad_down,
    )


def solution(mesh):
    placed = (
        P("dp", "tensor"),
        P("dp", "tensor"),
        P(),
        P(),
        P(None, "tensor"),
        P(None, "tensor"),
        P(None, "tensor"),
        P(None, "tensor"),
        P("tensor", None),
        P(),
        P(),
        P(None, "tensor"),
        P(None, "tensor"),
        P("tensor", None),
        P("tensor"),
        P(),
        P(),
    )
    wires = Wires(mesh.shape["dp"], mesh.shape["tensor"])
    return jax.shard_map(
        functools.partial(local, wires),
        mesh=mesh,
        in_specs=placed,
        out_specs=(
            P("dp", "tensor"),
            P("dp", "tensor"),
            P(),
            P(),
            P(None, "tensor"),
            P(None, "tensor"),
            P(None, "tensor"),
            P(None, "tensor"),
            P("tensor", None),
            P(),
            P(),
            P(None, "tensor"),
            P(None, "tensor"),
            P("tensor", None),
        ),
        check_vma=False,
    )
```

```python
import functools
import math

import jax
import jax.numpy as jnp
from jax import lax
from jax.experimental import pallas as pl
from jax.experimental.pallas import tpu as pltpu
from jax.sharding import PartitionSpec as P


norm_eps = 1e-05


def layout(seq_lens, seq_owner, device, row_count):
    owned_mask = (seq_owner == device).astype(jnp.int32)
    seq_count = seq_lens * owned_mask
    starts = jnp.cumsum(seq_count, dtype=jnp.int32) - seq_count
    row_ids = jnp.arange(row_count, dtype=jnp.int32)[:, None]
    inside = ((row_ids >= starts[None, :]) & (row_ids < (starts + seq_count)[None, :])).astype(
        jnp.int32
    )
    seq_numbers = jnp.arange(seq_count.shape[0], dtype=jnp.int32)
    segment = jnp.sum(inside * (seq_numbers[None, :] + 1), axis=1, dtype=jnp.int32) - 1
    position = jnp.sum(inside * (row_ids - starts[None, :]), axis=1, dtype=jnp.int32)
    return (segment, position)


def xpos_tables(position, half_dim):
    freq_index = jnp.arange(half_dim, dtype=jnp.float32)
    angle_rate = 10000.0 ** (-freq_index / half_dim)
    zeta_base = (freq_index / half_dim + 0.4) / 1.4
    pos_col = position.astype(jnp.float32)[:, None]
    angles = pos_col * angle_rate[None, :]
    growth = jnp.exp(jnp.log(zeta_base)[None, :] * pos_col / 512.0)
    return (jnp.cos(angles), jnp.sin(angles), growth)


def decay_mask(segment, position, rates):
    row_count = segment.shape[0]
    same_seq = (segment[:, None] == segment[None, :]) & (segment[:, None] >= 0)
    row_ids = jnp.arange(row_count, dtype=jnp.int32)
    allowed = same_seq & (row_ids[:, None] >= row_ids[None, :])
    distance = jnp.where(allowed, (position[:, None] - position[None, :]).astype(jnp.float32), 0.0)
    return jnp.where(allowed[None], jnp.exp(-rates[:, None, None] * distance[None]), 0.0)


def nt(left, right):
    return lax.dot_general(left, right, (((1,), (1,)), ((), ())), preferred_element_type=jnp.float32)


def tn(left, right):
    return lax.dot_general(left, right, (((0,), (0,)), ((), ())), preferred_element_type=jnp.float32)


def nn(left, right):
    return jnp.dot(left, right, preferred_element_type=jnp.float32)


anywhere = pl.BlockSpec(memory_space=pl.ANY)
in_vmem = pl.BlockSpec(memory_space=pltpu.VMEM)
in_smem = pl.BlockSpec(memory_space=pltpu.SMEM)
bf16, f32 = jnp.bfloat16, jnp.float32


def shape_of(dims, dtype):
    return jax.ShapeDtypeStruct(dims, dtype)


def call(kernel, operands, specs, outs, scratch=(), flops=0, mib=62):
    moved = sum(one.size * one.dtype.itemsize for one in operands)
    moved += sum(math.prod(one.shape) * jnp.dtype(one.dtype).itemsize for one in outs)
    return pl.pallas_call(
        kernel,
        in_specs=list(specs),
        out_specs=[in_vmem] * len(outs),
        out_shape=list(outs),
        scratch_shapes=list(scratch),
        compiler_params=pltpu.CompilerParams(vmem_limit_bytes=mib * 2**20),
        cost_estimate=pl.CostEstimate(flops=flops, bytes_accessed=moved, transcendentals=0),
    )(*operands)


def loads(sources, buffers, sems):
    copies = [
        pltpu.make_async_copy(source, buffer, sems.at[at])
        for at, (source, buffer) in enumerate(zip(sources, buffers))
    ]
    for one in copies:
        one.start()
    return copies


def row_loop(rows, step, body):
    for begin in range(0, rows, step):
        body(slice(begin, begin + step))


def mean_of(values):
    return jnp.mean(values, axis=-1, keepdims=True)


def norm_parts(values):
    centred = values - mean_of(values)
    inv_std = lax.rsqrt(mean_of(centred * centred) + norm_eps)
    return centred * inv_std, inv_std


def norm_back_rows(near, far, source, gain, base, out, small_out):
    step = 16
    small_gain = small_bias = 0.0
    for begin in range(0, near.shape[0], step):
        at = slice(begin, begin + step)
        upstream = near[at, :].astype(f32) + far[at, :].astype(f32)
        hat, inv_std = norm_parts(source(at))
        small_gain = small_gain + fold_rows(upstream * hat)
        small_bias = small_bias + fold_rows(upstream)
        scaled = upstream * gain[...]
        out[at, :] = base(at) + inv_std * (scaled - mean_of(scaled) - hat * mean_of(scaled * hat))
    small_out[0:1, :] = jnp.sum(small_gain, axis=0, keepdims=True)
    small_out[1:2, :] = jnp.sum(small_bias, axis=0, keepdims=True)


def fold_rows(values):
    total = values[:8]
    for at in range(8, values.shape[0], 8):
        total = total + values[at : at + 8]
    return total


def put_columns(pieces, places, out):
    width = pieces[0].shape[1]
    for at, piece in enumerate(pieces):
        out[:, pl.ds(pl.multiple_of(places[at] * width, width), width)] = piece[...]


def cotangent_kernel(count, places, *refs):
    pieces, (live, weight_at, grads_out, back_out, weight, sems) = refs[:count], refs[count:]
    ready = loads((weight_at,), (weight,), sems)
    put_columns(pieces, places, grads_out)

    def body(rows):
        grads = grads_out[rows, :]
        grads_out[rows, :] = jnp.where(live[rows, :] > 0, grads, jnp.zeros_like(grads))

    row_loop(grads_out.shape[0], 32, body)
    ready[0].wait()
    back_out[...] = nt(weight[...], grads_out[...])


def cotangent(pieces, places, live, weight):
    rows, features = pieces[0].shape[0], len(pieces) * pieces[0].shape[1]
    return call(
        functools.partial(cotangent_kernel, len(pieces)),
        (places, *pieces, live[:, None], weight),
        [in_smem] + [in_vmem] * (len(pieces) + 1) + [anywhere],
        [shape_of((rows, features), bf16), shape_of((weight.shape[0], rows), f32)],
        [pltpu.VMEM(weight.shape, bf16), pltpu.SemaphoreType.DMA((1,))],
        flops=2 * rows * weight.size,
    )


def silu(values):
    return values / (1.0 + jnp.exp(-values))


def retention_kernel(heads, count, places, *refs):
    pieces, refs = refs[:count], refs[count:]
    gain, bias, cosine, sine, growth, mask, wq_at, wk_at, wv_at, wg_at, wo_at = refs[:11]
    x_out, sent, qx_out, kx_out, v_out, g_out, y_out, inv_out, weights_out, part_out = refs[11:21]
    act, wq, wk, wv, wg, wo, ret, sems = refs[21:]
    ready = loads((wq_at, wk_at, wv_at, wg_at, wo_at), (wq, wk, wv, wg, wo), sems)
    put_columns(pieces, places, x_out)

    def normalize(rows):
        hat, _ = norm_parts(x_out[rows, :].astype(f32))
        act[rows, :] = (hat * gain[...] + bias[...]).astype(bf16)

    row_loop(x_out.shape[0], 32, normalize)
    put_blocks(act, sent, 0)
    begin = act.shape[1] // 128 * act.shape[0]
    key_dim, val_dim = wq.shape[1] // heads, wv.shape[0] // heads
    half = key_dim // 2
    grow = growth[...]
    shrink = 1.0 / grow * key_dim ** (-0.5)
    cos, sin = cosine[...], sine[...]
    for ready_at, weight, factor, out in ((0, wq, grow, qx_out), (1, wk, shrink, kx_out)):
        ready[ready_at].wait()
        full = nn(act[...], weight[...])
        for head in range(heads):
            low = full[:, head * key_dim : head * key_dim + half]
            high = full[:, head * key_dim + half : (head + 1) * key_dim]
            out[:, head * key_dim : head * key_dim + half] = ((low * cos - high * sin) * factor).astype(bf16)
            out[:, head * key_dim + half : (head + 1) * key_dim] = ((low * sin + high * cos) * factor).astype(bf16)
    ready[2].wait()
    v_out[...] = nt(wv[...], act[...]).astype(bf16)
    for head in range(heads):
        keys = slice(head * key_dim, (head + 1) * key_dim)
        vals = slice(head * val_dim, (head + 1) * val_dim)
        weights = (nt(qx_out[:, keys], kx_out[:, keys]) * mask[head]).astype(bf16)
        weights_out[head] = weights
        ret[vals, :] = nt(v_out[vals, :], weights)
    ready[3].wait()
    g_out[...] = nt(wg[...], act[...])
    for head in range(heads):
        vals = slice(head * val_dim, (head + 1) * val_dim)
        mean = jnp.mean(ret[vals, :], axis=0, keepdims=True)
        centred = ret[vals, :] - mean
        inv_std = lax.rsqrt(jnp.mean(centred * centred, axis=0, keepdims=True) + norm_eps)
        inv_out[head : head + 1, :] = inv_std
        y = centred * inv_std
        y_out[vals, :] = y
        sent[begin + vals.start : begin + vals.stop, :] = (silu(g_out[vals, :]) * y).astype(bf16)
    ready[4].wait()
    part_out[...] = tn(sent[begin:, :], wo[...]).astype(bf16)


def retention(pieces, places, gain, bias, cosine, sine, growth, mask, wq, wk, wv, wg, wo):
    heads, rows, _ = mask.shape
    features, keys, vals = wq.shape[0], wq.shape[1], wv.shape[0]
    weights = (wq, wk, wv, wg, wo)
    return call(
        functools.partial(retention_kernel, heads, len(pieces)),
        (places, *pieces, gain[None], bias[None], cosine, sine, growth, mask, *weights),
        [in_smem] + [in_vmem] * (len(pieces) + 6) + [anywhere] * 5,
        [
            shape_of((rows, features), bf16),
            shape_of((features // 128 * rows + vals, 128), bf16),
            shape_of((rows, keys), bf16),
            shape_of((rows, keys), bf16),
            shape_of((vals, rows), bf16),
            shape_of((vals, rows), f32),
            shape_of((vals, rows), f32),
            shape_of((heads, rows), f32),
            shape_of((heads, rows, rows), bf16),
            shape_of((rows, features), bf16),
        ],
        [pltpu.VMEM((rows, features), bf16)]
        + [pltpu.VMEM(one.shape, bf16) for one in weights]
        + [pltpu.VMEM((vals, rows), f32), pltpu.SemaphoreType.DMA((5,))],
        flops=2 * rows * sum(one.size for one in weights),
        mib=62,
    )


def blocks_to_rows(ref, rows, first, count):
    return jnp.concatenate([ref[at * rows : (at + 1) * rows, :] for at in range(first, first + count)], axis=1)


def put_blocks(values, out, begin):
    rows, width = values.shape
    for at in range(width // 128):
        out[begin + at * rows : begin + (at + 1) * rows, :] = values[:, at * 128 : (at + 1) * 128]


def gelu_and_slope(values):
    scale = (2.0 / jnp.pi) ** 0.5
    square = values * values
    reach = jnp.tanh(scale * (values + 0.044715 * (values * square)))
    half_one = 0.5 * (1.0 + reach)
    slope = half_one + 0.5 * values * (1.0 - reach * reach) * (scale * (1.0 + 3 * 0.044715 * square))
    return values * half_one, slope


def mlp_kernel(x, near, far, gain, bias, back_hidden, wg_at, wu_at, resid_out, sent, part_out, act, wg, wu, gate, up, sems):
    ready = loads((wg_at, wu_at), (wg, wu), sems)
    rows, features = act.shape
    units = wg.shape[0]
    begin = features // 128 * rows

    def normalize(at):
        resid = x[at, :].astype(f32) + (near[at, :].astype(f32) + far[at, :].astype(f32))
        resid_out[at, :] = resid
        hat, _ = norm_parts(resid)
        act[at, :] = (hat * gain[...] + bias[...]).astype(bf16)

    row_loop(rows, 32, normalize)
    put_blocks(act, sent, 0)
    ready[0].wait()
    gate[...] = nt(wg[...], act[...])
    ready[1].wait()
    up[...] = nt(wu[...], act[...])
    for row in range(0, units, 48):
        at = slice(row, row + 48)
        value, slope = gelu_and_slope(gate[at, :])
        linear, back = up[at, :], back_hidden[at, :]
        row += begin
        sent[row : row + 48, :] = (value * linear).astype(bf16)
        sent[row + units : row + units + 48, :] = (back * linear * slope).astype(bf16)
        sent[row + 2 * units : row + 2 * units + 48, :] = (back * value).astype(bf16)
    part = tn(sent[begin + units : begin + 2 * units, :], wg[...]) + tn(sent[begin + 2 * units :, :], wu[...])
    part_out[...] = part.astype(bf16)


def mlp(x, near, far, gain, bias, back_hidden, wg, wu):
    units, features = wg.shape
    rows = x.shape[0]
    tall = features // 128 * rows
    return call(
        mlp_kernel,
        (x, near, far, gain[None], bias[None], back_hidden, wg, wu),
        [in_vmem] * 6 + [anywhere] * 2,
        [
            shape_of((rows, features), f32),
            shape_of((tall + 3 * units, 128), bf16),
            shape_of((rows, features), bf16),
        ],
        [pltpu.VMEM((rows, features), bf16)]
        + [pltpu.VMEM(wg.shape, bf16)] * 2
        + [pltpu.VMEM((units, rows), f32)] * 2
        + [pltpu.SemaphoreType.DMA((2,))],
        flops=8 * rows * wg.size,
    )


def down_kernel(begin, group, place, sent_at, weight, resid_at, *refs):
    outs, (hidden, resid, sems) = refs[:group], refs[group:]
    units, width = weight.shape[0], resid.shape[1]
    ready = loads(
        (sent_at.at[begin : begin + units, :], resid_at.at[:, pl.ds(pl.multiple_of(place[0] * width, width), width)]),
        (hidden, resid),
        sems,
    )
    ready[0].wait()
    for at in range(group):
        columns = pl.ds(pl.multiple_of((place[0] ^ at) * width, width), width)
        part = tn(hidden[...], weight[:, columns]).astype(bf16)
        if at == 0:
            ready[1].wait()
            outs[0][...] = resid[...] + part.astype(f32)
        else:
            outs[at][...] = part


def down(place, group, sent, begin, weight, resid):
    units, rows, width = weight.shape[0], resid.shape[0], resid.shape[1] // group
    return call(
        functools.partial(down_kernel, begin, group),
        (place, sent, weight, resid),
        [in_smem, anywhere, in_vmem, anywhere],
        [shape_of((rows, width), f32)] + [shape_of((rows, width), bf16)] * (group - 1),
        [pltpu.VMEM((units, rows), bf16), pltpu.VMEM((rows, width), f32), pltpu.SemaphoreType.DMA((2,))],
        flops=2 * rows * weight.size,
    )


def retention_back_kernel(
    heads, near, far, grads, resid, gain, g, y, inv, v, weights, mask, qx, kx, cosine, sine, growth, wo_at,
    back_out, rb, small_out, sent, wo, back, sems,
):
    ready = loads((wo_at,), (wo,), sems)
    norm_back_rows(near, far, lambda at: resid[at, :], gain, lambda at: grads[at, :].astype(f32), back_out, small_out)
    rb[...] = back_out[...].astype(bf16)
    key_dim, val_dim = qx.shape[1] // heads, v.shape[0] // heads
    half = key_dim // 2
    all_vals, rows = heads * val_dim, rb.shape[0]
    grow = growth[...]
    shrink = 1.0 / grow * key_dim ** (-0.5)
    cos, sin = cosine[...], sine[...]
    ready[0].wait()
    back[...] = nt(wo[...], rb[...])
    for head in range(heads):
        vals = slice(head * val_dim, (head + 1) * val_dim)
        upstream, gate, norm = back[vals, :], g[vals, :], y[vals, :]
        logistic = 1.0 / (1.0 + jnp.exp(-gate))
        swish = gate * logistic
        slope = logistic + swish * (1.0 - logistic)
        sent[all_vals + head * val_dim : all_vals + (head + 1) * val_dim, :] = (upstream * norm * slope).astype(bf16)
        back_y = upstream * swish
        first = jnp.mean(back_y, axis=0, keepdims=True)
        second = jnp.mean(back_y * norm, axis=0, keepdims=True)
        back_ret = (inv[head : head + 1, :] * (back_y - first - norm * second)).astype(bf16)
        sent[vals, :] = nn(back_ret, weights[head]).astype(bf16)
        back_weights = (tn(back_ret, v[vals, :]) * mask[head]).astype(bf16)
        low, high = slice(head * key_dim, head * key_dim + half), slice(head * key_dim + half, (head + 1) * key_dim)
        keys = slice(head * key_dim, (head + 1) * key_dim)
        offset = heads * key_dim
        for grad, factor, begin in (
            (nn(back_weights, kx[:, keys]), grow, 0),
            (tn(back_weights, qx[:, keys]), shrink, offset),
        ):
            one, two = grad[:, :half], grad[:, half:]
            put_blocks(((one * cos + two * sin) * factor).astype(bf16), sent, 2 * all_vals + (begin + low.start) // 128 * rows)
            put_blocks(((two * cos - one * sin) * factor).astype(bf16), sent, 2 * all_vals + (begin + high.start) // 128 * rows)


def retention_back(near, far, grads, resid, gain, g, y, inv, v, weights, mask, qx, kx, cosine, sine, growth, wo):
    heads, rows, _ = mask.shape
    vals, keys, features = v.shape[0], qx.shape[1], wo.shape[1]
    return call(
        functools.partial(retention_back_kernel, heads),
        (near, far, grads, resid, gain[None], g, y, inv, v, weights, mask, qx, kx, cosine, sine, growth, wo),
        [in_vmem] * 16 + [anywhere],
        [
            shape_of((rows, features), f32),
            shape_of((rows, features), bf16),
            shape_of((2, features), f32),
            shape_of((2 * vals + 2 * keys // 128 * rows, 128), bf16),
        ],
        [pltpu.VMEM(wo.shape, bf16), pltpu.VMEM((vals, rows), f32), pltpu.SemaphoreType.DMA((1,))],
        flops=2 * rows * wo.size,
    )


def first_back_kernel(sent, wq_at, wk_at, wv_at, wg_at, part_out, wq, wk, wv, wg, sems):
    ready = loads((wv_at, wg_at, wq_at, wk_at), (wv, wg, wq, wk), sems)
    rows, vals, keys = part_out.shape[0], wv.shape[0], wq.shape[1]
    count = keys // 128
    ready[0].wait()
    total = tn(sent[:vals, :], wv[...])
    ready[1].wait()
    total = total + tn(sent[vals : 2 * vals, :], wg[...])
    ready[2].wait()
    narrow = [sent[2 * vals + at * rows : 2 * vals + (at + 1) * rows, :] for at in range(2 * count)]
    total = total + nt(jnp.concatenate(narrow[:count], axis=1), wq[...])
    ready[3].wait()
    total = total + nt(jnp.concatenate(narrow[count:], axis=1), wk[...])
    part_out[...] = total.astype(bf16)


def first_back(sent, rows, wq, wk, wv, wg):
    features = wq.shape[0]
    weights = (wq, wk, wv, wg)
    return call(
        first_back_kernel,
        (sent, *weights),
        [in_vmem] + [anywhere] * 4,
        [shape_of((rows, features), bf16)],
        [pltpu.VMEM(one.shape, bf16) for one in weights] + [pltpu.SemaphoreType.DMA((4,))],
        flops=2 * rows * sum(one.size for one in weights),
        mib=62,
    )[0]


def first_norm_back_kernel(place, near, far, x, gain, back, out, small_out, full):
    norm_back_rows(near, far, lambda at: x[at, :].astype(f32), gain, lambda at: back[at, :], full, small_out)
    width = out.shape[1]
    out[...] = full[:, pl.ds(pl.multiple_of(place[0] * width, width), width)]


def first_norm_back(place, near, far, x, gain, back, width):
    rows, features = x.shape
    return call(
        first_norm_back_kernel,
        (place, near, far, x, gain[None], back),
        [in_smem] + [in_vmem] * 5,
        [shape_of((rows, width), f32), shape_of((2, features), f32)],
        [pltpu.VMEM((rows, features), f32)],
    )


def add_up(lefts, first, out, right):
    height = out.shape[0]
    tile = next(one for one in (288, 216, 144, 432, 16) if height % one == 0)
    for row in range(0, height, tile):
        rows = slice(first + row, first + row + tile)
        out[row : row + tile, :] = nn(jnp.concatenate([ref[rows, :] for ref in lefts], axis=1), right)


def stacked(refs):
    return jnp.concatenate([ref[...] for ref in refs], axis=0)


def stacked_blocks(refs, rows, first, count):
    return jnp.concatenate([blocks_to_rows(ref, rows, first, count) for ref in refs], axis=0)


def head_kernel(count, *refs):
    lefts, acts, grads = (refs[at * count : (at + 1) * count] for at in range(3))
    down_out, gate_out, up_out = refs[3 * count :]
    units, step = down_out.shape
    rows = grads[0].shape[0]
    add_up(lefts, 0, down_out, stacked(grads))
    right = stacked_blocks(acts, rows, 0, step // 128)
    add_up(lefts, units, gate_out, right)
    add_up(lefts, 2 * units, up_out, right)


def last_kernel(count, *refs):
    wide, narrow, acts = (refs[at * count : (at + 1) * count] for at in range(3))
    v_out, g_out, q_out, k_out = refs[3 * count :]
    vals, step = v_out.shape
    rows, keys = wide[0].shape[1], q_out.shape[1]
    right = stacked_blocks(acts, rows, 0, step // 128)
    add_up(wide, 0, v_out, right)
    add_up(wide, vals, g_out, right)
    for at, out in enumerate((q_out, k_out)):
        out[...] = tn(right, stacked_blocks(narrow, rows, at * keys // 128, keys // 128))


def out_kernel(count, *refs):
    gated, resid, out = refs[:count], refs[count : 2 * count], refs[2 * count]
    add_up(gated, 0, out, stacked(resid))


def kept(first, height, rows):
    return pl.BlockSpec((pl.Element(height), pl.Element(rows)), lambda j: (first, 0), pipeline_mode=pl.Buffered(1))


def grad_call(kernel, step, width, count, operands, specs, outs, out_specs, flops, mib):
    moved = sum(math.prod(one.shape) * 4 for one in outs) * 3 // 2
    return pl.pallas_call(
        functools.partial(kernel, count),
        grid=(width // step,),
        in_specs=[spec for spec in specs for _ in range(count)],
        out_specs=out_specs,
        out_shape=outs,
        compiler_params=pltpu.CompilerParams(vmem_limit_bytes=mib * 2**20),
        cost_estimate=pl.CostEstimate(flops=flops, bytes_accessed=moved, transcendentals=0),
    )(*operands)


def grads_head(mid, cot, units):
    count, (rows, width) = len(mid), cot[0].shape
    tall = width // 128 * rows
    step = min(512, width)
    return grad_call(
        head_kernel,
        step,
        width,
        count,
        (*mid, *mid, *cot),
        [
            kept(tall, 3 * units, rows),
            pl.BlockSpec((step // 128 * rows, 128), lambda j: (j, 0)),
            pl.BlockSpec((rows, step), lambda j: (0, j)),
        ],
        [shape_of((units, width), f32)] * 3,
        [pl.BlockSpec((units, step), lambda j: (0, j))] * 3,
        6 * units * rows * count * width,
        62,
    )


def grads_last(last, one, rows, width, vals, keys):
    count = len(one)
    step = min(512, width)
    return grad_call(
        last_kernel,
        step,
        width,
        count,
        (*last, *last, *one),
        [
            kept(0, 2 * vals, rows),
            kept(2 * vals, 2 * keys // 128 * rows, rows),
            pl.BlockSpec((step // 128 * rows, 128), lambda j: (j, 0)),
        ],
        [shape_of((vals, width), f32)] * 2 + [shape_of((width, keys), f32)] * 2,
        [pl.BlockSpec((vals, step), lambda j: (0, j))] * 2 + [pl.BlockSpec((step, keys), lambda j: (j, 0))] * 2,
        4 * (vals + keys) * rows * count * width,
        62,
    )


def grads_out(one, five, vals):
    count, (rows, width) = len(one), five[0].shape
    step = min(512, width)
    return grad_call(
        out_kernel,
        step,
        width,
        count,
        (*one, *five),
        [kept(width // 128 * rows, vals, rows), pl.BlockSpec((rows, step), lambda j: (0, j))],
        [shape_of((vals, width), f32)],
        [pl.BlockSpec((vals, step), lambda j: (0, j))],
        2 * vals * rows * count * width,
        62,
    )[0]


both_axes = ("dp", "tensor")


def swap_perm(dp_size, tensor_size, dp_masks, tensor_masks):
    pairs = []
    for dp_at in range(dp_size):
        core = dp_at % 2
        for t_at in range(tensor_size):
            source = dp_at * tensor_size + t_at
            target = (dp_at ^ dp_masks[core]) * tensor_size + (t_at ^ tensor_masks[core])
            pairs.append((source, target))
    return pairs


class Wires:
    def __init__(self, dp_size, tensor_size):
        self.dp_size, self.tensor_size = dp_size, tensor_size
        make = functools.partial(swap_perm, dp_size, tensor_size)
        self.ring = tensor_size == 4 and dp_size % 2 == 0
        self.square = dp_size == 8
        if self.ring:
            self.z_first, self.z_second = make((0, 0), (1, 3)), make((0, 0), (3, 1))
        if self.square:
            self.xy_first, self.xy_second = make((2, 4), (0, 0)), make((4, 2), (0, 0))
            self.x_only, self.y_only = make((2, 2), (0, 0)), make((4, 4), (0, 0))
            self.core = make((1, 1), (0, 0))

    def send(self, value, pairs):
        return lax.ppermute(value, both_axes, pairs)

    def gather_columns(self, shard):
        if not self.ring:
            pieces = lax.all_gather(shard, "tensor", axis=0, tiled=False)
            count = self.tensor_size
            return [pieces[at] for at in range(count)], jnp.arange(count, dtype=jnp.int32)
        t_at = lax.axis_index("tensor")
        odd = lax.axis_index("dp") % 2
        first = self.send(shard, self.z_first)
        second = self.send(shard, self.z_second)
        far = self.send(first, self.z_second)
        near = 1 + 2 * odd
        places = jnp.stack([t_at, t_at ^ near, t_at ^ near ^ 2, t_at ^ 2])
        return [shard, first, second, far], places

    def gather_columns_at_once(self, shard):
        if not self.ring:
            return self.gather_columns(shard)
        t_at = lax.axis_index("tensor")
        pieces = [shard]
        for mask in range(1, self.tensor_size):
            pairs = swap_perm(self.dp_size, self.tensor_size, (0, 0), (mask, mask))
            pieces.append(self.send(shard, pairs))
        return pieces, jnp.stack([t_at ^ mask for mask in range(self.tensor_size)])

    def sum_over_tensor(self, mine):
        if not self.ring:
            return lax.psum(mine, "tensor"), jnp.zeros_like(mine)
        other = self.send(mine, self.z_first)
        pair = (mine.astype(f32) + other.astype(f32)).astype(bf16)
        return pair, self.send(pair, self.z_second)

    def add_shares(self, total, shares):
        for mask, share in enumerate(shares, 1):
            pairs = swap_perm(self.dp_size, self.tensor_size, (0, 0), (mask, mask))
            total = total + self.send(share, pairs).astype(f32)
        return total

    def rows_of_all(self, block):
        if not self.square:
            stacked = lax.all_gather(block, "dp", axis=0, tiled=False)
            return [stacked[at] for at in range(self.dp_size)]
        first = self.send(block, self.xy_first)
        second = self.send(block, self.xy_second)
        far = self.send(first, self.xy_second)
        near = [block, first, second, far]
        return near + [self.send(piece, self.core) for piece in near]

    def sum_small(self, vector):
        if not self.square:
            return lax.psum(vector, "dp")
        for pairs in (self.core, self.x_only, self.y_only):
            vector = vector + self.send(vector, pairs)
        return vector


def local(wires, *arrays):
    return layer(wires, *arrays)


def layer(
    wires,
    tokens,
    grad_out,
    ln1_gain,
    ln1_bias,
    w_query,
    w_key,
    w_value,
    w_gate_ret,
    w_out,
    ln2_gain,
    ln2_bias,
    w_gate_mlp,
    w_up,
    w_down,
    decay_rate,
    seq_lens,
    seq_owner,
):
    row_count, col_count = tokens.shape
    features = w_query.shape[0]
    local_heads = decay_rate.shape[0]
    key_dim = w_query.shape[1] // local_heads
    w_value, w_gate_ret, w_gate_mlp, w_up = w_value.T, w_gate_ret.T, w_gate_mlp.T, w_up.T
    units, vals, keys = w_up.shape[0], w_value.shape[0], w_query.shape[1]
    tensor_at = lax.axis_index("tensor")
    segment, position = layout(seq_lens, seq_owner, lax.axis_index("dp"), row_count)
    live = (segment >= 0).astype(f32)
    pieces, places = wires.gather_columns(tokens)
    cosine, sine, growth = xpos_tables(position, key_dim // 2)
    mask = decay_mask(segment, position, decay_rate)

    x_full, sent_one, qx, kx, value, gate, y_norm, inv_group, weights, out_part = retention(
        pieces, places, ln1_gain, ln1_bias, cosine, sine, growth, mask, w_query, w_key, w_value, w_gate_ret, w_out
    )
    pieces, places = wires.gather_columns_at_once(grad_out)
    near, far = wires.sum_over_tensor(out_part)
    all_one = wires.rows_of_all(sent_one)
    grads, back_hidden = cotangent(pieces, places, live, w_down)
    all_cot = wires.rows_of_all(grads)
    resid, mid, partial_two = mlp(x_full, near, far, ln2_gain, ln2_bias, back_hidden, w_gate_mlp, w_up)
    near, far = wires.sum_over_tensor(partial_two)
    all_mid = wires.rows_of_all(mid)
    tall = features // 128 * row_count
    own, *shares = down(tensor_at[None], features // col_count, mid, tall, w_down, resid)
    block_out = wires.add_shares(own, shares)
    back_resid, resid_b, small_two, last = retention_back(
        near, far, grads, resid, ln2_gain,
        gate, y_norm, inv_group, value, weights, mask, qx, kx, cosine, sine, growth, w_out,
    )
    all_five = wires.rows_of_all(resid_b)
    all_last = wires.rows_of_all(last)
    partial_one = first_back(last, row_count, w_query, w_key, w_value, w_gate_ret)
    near, far = wires.sum_over_tensor(partial_one)
    grad_tokens, small_one = first_norm_back(tensor_at[None], near, far, x_full, ln1_gain, back_resid, col_count)
    small = wires.sum_small(jnp.concatenate([small_one, small_two], axis=0))

    grad_down, grad_gate_mlp, grad_up = grads_head(all_mid, all_cot, units)
    grad_v, grad_g, grad_q, grad_k = grads_last(all_last, all_one, row_count, features, vals, keys)
    grad_out_w = grads_out(all_one, all_five, vals)
    return (
        block_out,
        grad_tokens,
        small[0],
        small[1],
        grad_q,
        grad_k,
        grad_v.T,
        grad_g.T,
        grad_out_w,
        small[2],
        small[3],
        grad_gate_mlp.T,
        grad_up.T,
        grad_down,
    )


def solution(mesh):
    placed = (
        P("dp", "tensor"),
        P("dp", "tensor"),
        P(),
        P(),
        P(None, "tensor"),
        P(None, "tensor"),
        P(None, "tensor"),
        P(None, "tensor"),
        P("tensor", None),
        P(),
        P(),
        P(None, "tensor"),
        P(None, "tensor"),
        P("tensor", None),
        P("tensor"),
        P(),
        P(),
    )
    wires = Wires(mesh.shape["dp"], mesh.shape["tensor"])
    return jax.shard_map(
        functools.partial(local, wires),
        mesh=mesh,
        in_specs=placed,
        out_specs=(
            P("dp", "tensor"),
            P("dp", "tensor"),
            P(),
            P(),
            P(None, "tensor"),
            P(None, "tensor"),
            P(None, "tensor"),
            P(None, "tensor"),
            P("tensor", None),
            P(),
            P(),
            P(None, "tensor"),
            P(None, "tensor"),
            P("tensor", None),
        ),
        check_vma=False,
    )
```
